512 devices in a mesh: tok: 32 (over z_hi, y), exp: 16 (over z_lo, x, core).
Axes of the slice: x: 4, y: 8, z: 8 (z_hi: 4, z_lo: 2; z = z_hi * 2 + z_lo), core: 2. Of those that a mesh axis runs over, the one named last changes fastest.
Arguments:
- tokens: bfloat16 [8192, 4096], P('tok', 'exp'), may hold values from -6 to 6
- w_gate: bfloat16 [4096, 8192], P('tok', 'exp'), may hold values from -0.09375 to 0.09375
- w_up: bfloat16 [4096, 8192], P('tok', 'exp'), may hold values from -0.09375 to 0.09375
- w_down: bfloat16 [8192, 4096], P('exp', 'tok'), may hold values from -0.0625 to 0.0625
- pattern: int32 [64], P('tok'), may hold values from 0 to 1, as said below
- gate_code: int32 [8192], P('tok'), may hold values from 1 to 255
Outputs:
- moe_out: bfloat16 [8192, 4096], P('tok', 'exp')
The draws below stay inside these ranges and needn't reach their ends.
Inputs may be any that keep to these rules, and one draw needn't show every extreme that they name: pattern holds 0 or 1 for each token block; in each aligned run of 2 blocks at most half are 1, and in every draw some run has exactly half.
All inputs are finite; a program needn't handle non-finite values.
Results may differ from the reference program's by a relative error of at most 0.0049.
Values may be sent and summed in bfloat16 or wider, within the bound.
No kernel may reach another device: no remote copies, remote signals or barrier semaphores. Data moves between devices by JAX's collectives and lax.ppermute only.
A program may use at most 64 MiB of HBM per device.

```python
import jax
import jax.numpy as jnp
from jax import lax

D = 4096
FF = 8192
BLOCK = 128
TOK_DEV = 256
TOKENS = 8192
NBLOCKS = 64


def draw_pattern(key, part):
    per_run = TOK_DEV // BLOCK
    runs = NBLOCKS // per_run
    most_live = per_run // 2
    first_key, second_key, third_key = jax.random.split(jax.random.fold_in(key, 17), 3)
    counts = jax.random.randint(first_key, (runs,), 0, most_live + 1)
    busiest = jax.random.randint(second_key, (), 0, runs)
    counts = jnp.where(jnp.arange(runs) == busiest, most_live, counts)
    ranks = jax.vmap(lambda one_key: jax.random.permutation(one_key, per_run))(jax.random.split(third_key, runs))
    return (ranks < counts[:, None]).astype(jnp.int32).reshape(NBLOCKS)


def set_ends(values, rng, smallest, largest):
    longest = values.shape.index(max(values.shape))
    spots = []
    for shift in (0, 1):
        where = [jax.random.randint(jax.random.fold_in(rng, axis), (), 0, length) for axis, length in enumerate(values.shape)]
        where[longest] = (where[longest] + shift) % values.shape[longest]
        spots.append(tuple(where))
    return values.at[spots[0]].set(smallest).at[spots[1]].set(largest)


def block_levels(own_key, shape, pieces, low, high):
    loudness, own = 1.0, jax.random.fold_in(own_key, 6)
    for axis_at, blocks in pieces:
        heights = jnp.exp(jax.random.uniform(jax.random.fold_in(own, axis_at), (blocks,), jnp.float32, low / len(pieces), high / len(pieces)))
        loudness = loudness * jnp.repeat(heights, shape[axis_at] // blocks).reshape([-1 if axis == axis_at else 1 for axis in range(len(shape))])
    return loudness


def gaussian(key, extent, width, bound, cuts=(), kind=jnp.bfloat16):
    values = jax.random.normal(key, extent, jnp.float32) * width
    if len(cuts) > 0:
        values = block_levels(key, extent, cuts, -0.22, 0.18) * values
    return jnp.clip(values, min=-bound, max=bound).astype(kind)


def setup_inputs(seed: int = 0) -> dict:
    arg_keys = jax.random.split(jax.random.key(seed), 7)
    tokens = gaussian(arg_keys[0], (TOKENS, D), 1.0, 6.0, ((0, 32), (1, 16)))
    w_gate = gaussian(arg_keys[1], (D, FF), D ** -0.5, 0.09375, ((0, 32), (1, 16)))
    w_up = gaussian(arg_keys[2], (D, FF), D ** -0.5, 0.09375, ((0, 32), (1, 16)))
    w_down = gaussian(arg_keys[3], (FF, D), FF ** -0.5, 0.0625, ((0, 16), (1, 32)))
    pattern = draw_pattern(jax.random.fold_in(arg_keys[6], 71), 0)
    gate_code = set_ends(jax.random.randint(arg_keys[5], (TOKENS,), 1, 256), jax.random.fold_in(arg_keys[5], 1), 1, 255).astype(jnp.int32)
    return dict(tokens=tokens, w_gate=w_gate, w_up=w_up, w_down=w_down, pattern=pattern, gate_code=gate_code)


def reference(tokens, w_gate, w_up, w_down, pattern, gate_code):
    def one_block(block_index):
        start = (block_index * BLOCK).astype(jnp.int32)
        rows_here = lax.dynamic_slice_in_dim(tokens, start, BLOCK, 0)
        codes = lax.dynamic_slice_in_dim(gate_code, start, BLOCK, 0)
        flag = pattern[block_index]
        row_scale = (codes.astype(jnp.float32) / 256.0 * flag.astype(jnp.float32)).astype(jnp.bfloat16)

        def compute(operand):
            gate_proj = jnp.dot(operand, w_gate, preferred_element_type=jnp.float32)
            up_proj = jnp.dot(operand, w_up, preferred_element_type=jnp.float32)
            hidden = (jax.nn.silu(gate_proj) * up_proj).astype(jnp.bfloat16)
            return jnp.dot(hidden, w_down, preferred_element_type=jnp.float32)

        def skipped(operand):
            return jnp.zeros((BLOCK, D), jnp.float32)

        summed = lax.cond(flag > 0, compute, skipped, rows_here)
        return (row_scale.astype(jnp.float32)[:, None] * summed).astype(jnp.bfloat16)

    blocks = lax.map(one_block, jnp.arange(NBLOCKS, dtype=jnp.int32))
    return blocks.reshape(NBLOCKS * BLOCK, D)
```

```python
import jax
import jax.numpy as jnp
from jax import lax
from jax.sharding import Mesh
from jax.sharding import PartitionSpec as P

TOK = ("zh", "y")
EXP = ("zl", "x", "c")
F32, BF16 = jnp.float32, jnp.bfloat16


def per_device(tokens, w_gate, w_up, w_down, pattern, gate_code):
    zh = lax.axis_index("zh")
    core = lax.axis_index("c")
    row_count, width = tokens.shape
    block_count = pattern.shape[0]
    block_rows = row_count // block_count
    hidden_count = w_gate.shape[1]
    groups = lax.axis_size("zh")
    quarter = lax.axis_size(EXP) // groups

    both = lax.all_gather(jnp.concatenate([w_gate, w_up], 1), "y", axis=0, tiled=True)

    chosen = jnp.where(pattern[0] > 0, 0, 1)
    live = pattern[chosen] > 0
    rows = lax.dynamic_slice_in_dim(tokens, chosen * block_rows, block_rows, 0)
    codes = lax.dynamic_slice_in_dim(gate_code, chosen * block_rows, block_rows, 0)
    row_scale = (codes.astype(F32) / 256.0 * live.astype(F32)).astype(BF16)
    scale_rows = jnp.zeros((8, width), BF16).at[0, :block_rows].set(row_scale)
    carried = jnp.concatenate([rows, scale_rows], 0)

    size = lax.axis_size(EXP)
    swap = []
    for z in range(groups):
        for a in range(groups):
            for b in range(quarter):
                swap.append((z * size + a * quarter + b, a * size + z * quarter + b))
    carried = lax.ppermute(carried, ("zh",) + EXP, swap)
    scale = carried[block_rows, :block_rows].astype(F32)
    rows = carried[:block_rows]

    chips = lax.all_gather(rows, ("zl", "x"), axis=0, tiled=False)
    other = lax.ppermute(chips, "c", [(0, 1), (1, 0)])
    first = jnp.where(core == 0, chips, other)
    second = jnp.where(core == 0, other, chips)
    lhs = jnp.stack([first, second], 1).reshape(groups, quarter, block_rows, width)
    lhs = lhs.transpose(0, 2, 1, 3).reshape(groups * block_rows, quarter * width)

    down = lax.all_gather(w_down, "y", axis=1, tiled=True)

    product = jnp.dot(lhs, both, preferred_element_type=F32)
    sent = product.astype(BF16).reshape(groups, block_rows, 2 * hidden_count)
    got = lax.all_to_all(sent, "zh", split_axis=0, concat_axis=0, tiled=True)
    own = lax.dynamic_slice_in_dim(product, zh * block_rows, block_rows, 0)
    total = jnp.zeros_like(own)
    for k in range(groups):
        total = total + jnp.where(k == zh, own, got[k].astype(F32))
    hidden = (jax.nn.silu(total[:, :hidden_count]) * total[:, hidden_count:]).astype(BF16)

    hidden = lax.all_gather(hidden, "zh", axis=0, tiled=True)
    part = jnp.dot(hidden, down, preferred_element_type=F32).astype(BF16)
    part = part.reshape(groups, block_rows, quarter, width).transpose(0, 2, 1, 3)
    part = part.reshape(groups * quarter, block_rows, width)
    parts = lax.all_to_all(part, EXP, split_axis=0, concat_axis=0, tiled=True)
    summed = jnp.sum(parts.astype(F32), 0)
    result = (scale[:, None] * summed).astype(BF16)
    result = lax.ppermute(result, ("zh",) + EXP, swap)

    outs = []
    for block_index in range(block_count):
        keep = jnp.logical_and(chosen == block_index, live)
        outs.append(jnp.where(keep, result, jnp.zeros_like(result)))
    return jnp.concatenate(outs, 0)


def solution(mesh):
    wide = Mesh(mesh.devices.reshape(4, 8, 2, 4, 2), ("zh", "y", "zl", "x", "c"))
    in_specs = (
        P(TOK, EXP),
        P(TOK, EXP),
        P(TOK, EXP),
        P(EXP, TOK),
        P(TOK),
        P(TOK),
    )
    return jax.shard_map(
        per_device, mesh=wide, in_specs=in_specs, out_specs=P(TOK, EXP), check_vma=False
    )
```

```python
import jax
import jax.numpy as jnp
from jax import lax
from jax.experimental import pallas as pl
from jax.experimental.pallas import tpu as pltpu
from jax.sharding import Mesh
from jax.sharding import PartitionSpec as P

TOK = ("zh", "y")
EXP = ("zl", "x", "c")
F32, BF16 = jnp.float32, jnp.bfloat16
LANES = 128


def pack(w_gate, w_up, w_down):
    rows, cols = w_gate.shape
    panels = cols // LANES

    def body(gate_ref, up_ref, down_ref, out_ref):
        for j in range(panels):
            out_ref[j] = gate_ref[:, j * LANES : (j + 1) * LANES]
            out_ref[panels + j] = up_ref[:, j * LANES : (j + 1) * LANES]
            out_ref[2 * panels + j] = down_ref[j * rows : (j + 1) * rows]

    return pl.pallas_call(
        body,
        out_shape=jax.ShapeDtypeStruct((3 * panels, rows, LANES), BF16),
        name="pack",
    )(w_gate, w_up, w_down)


def first_product(where, mine, theirs, weights):
    groups, lows, rows, width = mine.shape
    ranks, panels, depth, _ = weights.shape
    used = panels // 3 * 2
    wide = 2 * LANES
    span = width // depth

    def body(where_ref, mine_ref, theirs_ref, w_ref, sent_ref, own_ref):
        acc = jnp.zeros((groups * rows, wide), F32)
        for low in range(lows):
            for flip, ref in enumerate((mine_ref, theirs_ref)):
                core = where_ref[1] if flip == 0 else 1 - where_ref[1]
                at = pl.ds((low * 2 + core) * span, span)
                rhs = jnp.concatenate([w_ref[at, i].reshape(width, LANES) for i in range(2)], 1)
                part = ref[:, low].reshape(groups * rows, width)
                acc = acc + jnp.dot(part, rhs, preferred_element_type=F32)
        sent_ref[...] = acc.astype(BF16).reshape(groups, rows, wide)
        for z in range(groups):

            @pl.when(where_ref[0] == z)
            def _(z=z):
                own_ref[...] = acc[z * rows : (z + 1) * rows]

    return pl.pallas_call(
        body,
        grid_spec=pltpu.PrefetchScalarGridSpec(
            num_scalar_prefetch=1,
            grid=(used // 2,),
            in_specs=[
                pl.BlockSpec(mine.shape, lambda j, s: (0, 0, 0, 0)),
                pl.BlockSpec(theirs.shape, lambda j, s: (0, 0, 0, 0)),
                pl.BlockSpec((ranks, 2, depth, LANES), lambda j, s: (0, j, 0, 0)),
            ],
            out_specs=[
                pl.BlockSpec((groups, rows, wide), lambda j, s: (0, 0, j)),
                pl.BlockSpec((rows, wide), lambda j, s: (0, j)),
            ],
        ),
        out_shape=[
            jax.ShapeDtypeStruct((groups, rows, used * LANES), BF16),
            jax.ShapeDtypeStruct((rows, used * LANES), F32),
        ],
        cost_estimate=pl.CostEstimate(
            flops=2 * groups * rows * ranks * depth * used * LANES, bytes_accessed=5 << 20, transcendentals=0
        ),
        name="first_product",
    )(where, mine, theirs, weights)


def second_product(where, hidden, near, far):
    rows, hidden_count = hidden.shape
    ranks, others = far.shape[:2]
    groups = others + 1
    panels = hidden_count // LANES

    def body(where_ref, hidden_ref, near_ref, far_ref, out_ref):
        value = hidden_ref[...]
        for s in range(groups):
            if s == 0:
                halves = [near_ref[i].reshape(hidden_count, LANES) for i in range(2)]
            else:
                halves = [far_ref[i, s - 1] for i in range(2)]
            part = jnp.dot(value, jnp.concatenate(halves, 1), preferred_element_type=F32)
            out_ref[lax.rem(where_ref[0] + s, groups), 0] = part.astype(BF16)

    return pl.pallas_call(
        body,
        grid_spec=pltpu.PrefetchScalarGridSpec(
            num_scalar_prefetch=1,
            grid=(ranks // 2,),
            in_specs=[
                pl.BlockSpec(hidden.shape, lambda j, s: (0, 0)),
                pl.BlockSpec((2, panels) + near.shape[2:], lambda j, s: (j, 2, 0, 0)),
                pl.BlockSpec((2,) + far.shape[1:], lambda j, s: (j, 0, 0, 0)),
            ],
            out_specs=pl.BlockSpec((groups, 1, rows, 2 * LANES), lambda j, s: (0, j, 0, 0)),
        ),
        out_shape=jax.ShapeDtypeStruct((groups, ranks // 2, rows, 2 * LANES), BF16),
        cost_estimate=pl.CostEstimate(
            flops=2 * rows * hidden_count * groups * ranks * LANES, bytes_accessed=5 << 20, transcendentals=0
        ),
        name="second_product",
    )(where, hidden, near, far)


def per_device(tokens, w_gate, w_up, w_down, pattern, gate_code):
    zh = lax.axis_index("zh")
    row_count, width = tokens.shape
    block_count = pattern.shape[0]
    block_rows = row_count // block_count
    groups, ranks, size = lax.axis_size("zh"), lax.axis_size("y"), lax.axis_size(EXP)
    quarter = size // groups
    where = jnp.stack([zh, lax.axis_index("c")]).astype(jnp.int32)

    near = lax.all_gather(pack(w_gate, w_up, w_down), "y", axis=0, tiled=False)
    columns = lax.all_gather(w_down, "zh", axis=0, tiled=False)
    others = jnp.stack([lax.dynamic_index_in_dim(columns, (zh + s) % groups, keepdims=False) for s in range(1, groups)])
    far = lax.all_gather(others, "y", axis=0, tiled=False)

    chosen = jnp.where(pattern[0] > 0, 0, 1)
    rows = lax.dynamic_slice_in_dim(tokens, chosen * block_rows, block_rows, 0)
    flags = jnp.repeat(pattern, block_rows).astype(F32)
    row_scale = (gate_code.astype(F32) / 256.0 * flags).astype(BF16).astype(F32)

    swap = []
    for z in range(groups):
        for a in range(groups):
            for b in range(quarter):
                swap.append((z * size + a * quarter + b, a * size + z * quarter + b))
    rows = lax.ppermute(rows, ("zh",) + EXP, swap)
    chips = size // 2
    copies = jnp.broadcast_to(rows[None], (chips,) + rows.shape)
    mine = lax.all_to_all(copies, ("zl", "x"), split_axis=0, concat_axis=0, tiled=True)
    mine = mine.reshape(groups, chips // groups, block_rows, width)
    theirs = lax.ppermute(mine, "c", [(0, 1), (1, 0)])

    sent, own = first_product(where, mine, theirs, near)
    got = lax.all_to_all(sent, "zh", split_axis=0, concat_axis=0, tiled=True)
    total = own
    for k in range(groups):
        total = total + jnp.where(k == zh, 0.0, got[k].astype(F32))
    gate, up = jnp.split(total, 2, 1)
    hidden = (jax.nn.silu(gate) * up).astype(BF16)

    part = second_product(where, hidden, near, far)
    parts = lax.all_to_all(part.reshape(size, block_rows, width), EXP, split_axis=0, concat_axis=0, tiled=True)
    summed = jnp.sum(parts.astype(F32), 0)
    result = row_scale.reshape(block_count, block_rows, 1) * summed[None]
    return result.astype(BF16).reshape(row_count, width)


def solution(mesh):
    wide = Mesh(mesh.devices.reshape(4, 8, 2, 4, 2), ("zh", "y", "zl", "x", "c"))
    in_specs = (
        P(TOK, EXP),
        P(TOK, EXP),
        P(TOK, EXP),
        P(EXP, TOK),
        P(TOK),
        P(TOK),
    )
    return jax.shard_map(
        per_device, mesh=wide, in_specs=in_specs, out_specs=P(TOK, EXP), check_vma=False
    )
```

```python
import jax
import jax.numpy as jnp
from jax import lax
from jax.experimental import pallas as pl
from jax.experimental.pallas import tpu as pltpu
from jax.sharding import Mesh
from jax.sharding import PartitionSpec as P

TOK = ("zh", "y")
EXP = ("zl", "x", "c")
F32, BF16 = jnp.float32, jnp.bfloat16
LANES = 128


def first_product(where, mine, theirs, weights):
    groups, lows, rows, width = mine.shape
    depth, cols = weights.shape
    wide = 2 * LANES

    def body(where_ref, mine_ref, theirs_ref, w_ref, sent_ref, own_ref):
        acc = jnp.zeros((groups * rows, wide), F32)
        for low in range(lows):
            for flip, ref in enumerate((mine_ref, theirs_ref)):
                core = where_ref[1] if flip == 0 else 1 - where_ref[1]
                at = pl.ds(pl.multiple_of((low * 2 + core) * width, width), width)
                part = ref[:, low].reshape(groups * rows, width)
                acc = acc + jnp.dot(part, w_ref[at, :], preferred_element_type=F32)
        sent_ref[...] = acc.astype(BF16).reshape(groups, rows, wide)
        for z in range(groups):

            @pl.when(where_ref[0] == z)
            def _(z=z):
                own_ref[...] = acc[z * rows : (z + 1) * rows]

    return pl.pallas_call(
        body,
        grid_spec=pltpu.PrefetchScalarGridSpec(
            num_scalar_prefetch=1,
            grid=(cols // wide,),
            in_specs=[
                pl.BlockSpec(mine.shape, lambda j, s: (0, 0, 0, 0)),
                pl.BlockSpec(theirs.shape, lambda j, s: (0, 0, 0, 0)),
                pl.BlockSpec((depth, wide), lambda j, s: (0, j)),
            ],
            out_specs=[
                pl.BlockSpec((groups, rows, wide), lambda j, s: (0, 0, j)),
                pl.BlockSpec((rows, wide), lambda j, s: (0, j)),
            ],
        ),
        out_shape=[
            jax.ShapeDtypeStruct((groups, rows, cols), BF16),
            jax.ShapeDtypeStruct((rows, cols), F32),
        ],
        cost_estimate=pl.CostEstimate(
            flops=2 * groups * rows * depth * cols, bytes_accessed=5 << 20, transcendentals=0
        ),
        name="first_product",
    )(where, mine, theirs, weights)


def second_product(where, mine, theirs, down):
    rows, depth = mine[0].shape
    ranks, kinds = down.shape[:2]
    width = 2 * LANES

    def body(where_ref, a_ref, b_ref, c_ref, d_ref, down_ref, out_ref):
        core = where_ref[1]
        kind = jnp.where(where_ref[0] // 2 == core, 0, 1)
        left = jnp.concatenate([a_ref[...], b_ref[...]], 0)
        right = jnp.concatenate([c_ref[...], d_ref[...]], 0)
        part = jnp.dot(left, jnp.concatenate([down_ref[i, kind] for i in range(2)], 1), preferred_element_type=F32)
        part = part + jnp.dot(
            right, jnp.concatenate([down_ref[i, 1 - kind] for i in range(2)], 1), preferred_element_type=F32
        )
        out_ref[core, 0] = part[:rows].astype(BF16)
        out_ref[1 - core, 0] = part[rows:].astype(BF16)

    return pl.pallas_call(
        body,
        grid_spec=pltpu.PrefetchScalarGridSpec(
            num_scalar_prefetch=1,
            grid=(ranks // 2,),
            in_specs=[pl.BlockSpec((rows, depth), lambda j, s: (0, 0))] * 4
            + [pl.BlockSpec((2,) + down.shape[1:], lambda j, s: (j, 0, 0, 0))],
            out_specs=pl.BlockSpec((2, 1, rows, width), lambda j, s: (0, j % 2 * 2 + j // 2, 0, 0)),
        ),
        out_shape=jax.ShapeDtypeStruct((2, ranks // 2, rows, width), BF16),
        cost_estimate=pl.CostEstimate(
            flops=2 * 2 * rows * depth * kinds * ranks * LANES, bytes_accessed=4 << 20, transcendentals=0
        ),
        name="second_product",
    )(where, *mine, *theirs, down)


def per_device(tokens, w_gate, w_up, w_down, pattern, gate_code):
    zh = lax.axis_index("zh")
    row_count, width = tokens.shape
    block_count = pattern.shape[0]
    block_rows = row_count // block_count
    groups, size = lax.axis_size("zh"), lax.axis_size(EXP)
    quarter = size // groups
    where = jnp.stack([zh, lax.axis_index("c")]).astype(jnp.int32)

    both = lax.all_gather(jnp.concatenate([w_gate, w_up], 1), "y", axis=0, tiled=True)
    blocks = []
    for flip in range(2):
        moves = []
        for z in range(groups):
            for c in range(2):
                moves.append(((z % 2 + 2 * c) * 2 + (z // 2 + flip) % 2, z * 2 + c))
        blocks.append(lax.ppermute(w_down, ("zh", "c"), moves))
    down = lax.all_gather(jnp.stack(blocks), "y", axis=0, tiled=False)

    chosen = jnp.where(pattern[0] > 0, 0, 1)
    rows = lax.dynamic_slice_in_dim(tokens, chosen * block_rows, block_rows, 0)
    codes = lax.dynamic_slice_in_dim(gate_code, chosen * block_rows, block_rows, 0)
    live = pattern[chosen] > 0
    row_scale = (codes.astype(F32) / 256.0 * live.astype(F32)).astype(BF16)
    neighbour = [(i, i ^ 1) for i in range(groups)]
    swap = []
    for z in range(groups):
        for a in range(groups):
            for b in range(quarter):
                swap.append((z * size + a * quarter + b, a * size + z * quarter + b))
    rows = lax.ppermute(rows, ("zh",) + EXP, swap)
    chips = size // 2
    copies = jnp.broadcast_to(rows[None], (chips,) + rows.shape)
    mine = lax.all_to_all(copies, ("zl", "x"), split_axis=0, concat_axis=0, tiled=True)
    mine = mine.reshape(groups, chips // groups, block_rows, width)
    theirs = lax.ppermute(mine, "c", [(0, 1), (1, 0)])

    sent, own = first_product(where, mine, theirs, both)
    got = lax.all_to_all(sent, "zh", split_axis=0, concat_axis=0, tiled=True)
    total = own
    for k in range(groups):
        total = total + jnp.where(k == zh, 0.0, got[k].astype(F32))
    gate, up = jnp.split(total, 2, 1)
    hidden = (jax.nn.silu(gate) * up).astype(BF16)

    cores = [(0, 1), (1, 0)]
    row_scale, own = lax.optimization_barrier((row_scale, own))
    passed = lax.ppermute(row_scale, "zh", neighbour)
    hidden, row_scale, passed = lax.optimization_barrier((hidden, row_scale, passed))
    scale = jnp.where(lax.axis_index("zl") == lax.axis_index("c"), row_scale, passed)

    beside = lax.ppermute(hidden, "zh", neighbour)
    mine = (hidden, beside)
    theirs = (lax.ppermute(hidden, "c", cores), lax.ppermute(beside, "c", cores))
    part = second_product(where, mine, theirs, down)
    parts = lax.all_to_all(part.reshape(chips, block_rows, width), ("zl", "x"), split_axis=0, concat_axis=0, tiled=True)
    summed = jnp.sum(parts.astype(F32), 0)
    result = (scale.astype(F32)[:, None] * summed).astype(BF16)
    home = []
    for z in range(groups):
        for zl in range(2):
            for high in range(2):
                for low in range(2):
                    for c in range(2):
                        source = z * size + zl * 8 + (high * 2 + low) * 2 + c
                        target = z if zl == c else z ^ 1
                        home.append((source, target * size + c * 8 + (z % 2 * 2 + low) * 2 + high))
    result = lax.ppermute(result, ("zh",) + EXP, home)

    outs = []
    for block_index in range(block_count):
        keep = jnp.logical_and(chosen == block_index, live)
        outs.append(jnp.where(keep, result, jnp.zeros_like(result)))
    return jnp.concatenate(outs, 0)


def solution(mesh):
    wide = Mesh(mesh.devices.reshape(4, 8, 2, 4, 2), ("zh", "y", "zl", "x", "c"))
    in_specs = (
        P(TOK, EXP),
        P(TOK, EXP),
        P(TOK, EXP),
        P(EXP, TOK),
        P(TOK),
        P(TOK),
    )
    return jax.shard_map(
        per_device, mesh=wide, in_specs=in_specs, out_specs=P(TOK, EXP), check_vma=False
    )
```

```python
import jax
import jax.numpy as jnp
from jax import lax
from jax.experimental import pallas as pl
from jax.experimental.pallas import tpu as pltpu
from jax.sharding import Mesh
from jax.sharding import PartitionSpec as P

TOK = ("zh", "y")
EXP = ("zl", "x", "c")
F32, BF16 = jnp.float32, jnp.bfloat16
LANES = 128


def pack(w_gate, w_up, w_down):
    rows, cols = w_gate.shape
    panels = cols // LANES

    def body(gate_ref, up_ref, down_ref, out_ref):
        for j in range(panels):
            out_ref[j] = gate_ref[:, j * LANES : (j + 1) * LANES]
            out_ref[panels + j] = up_ref[:, j * LANES : (j + 1) * LANES]
            out_ref[2 * panels + j] = down_ref[j * rows : (j + 1) * rows]

    return pl.pallas_call(
        body,
        out_shape=jax.ShapeDtypeStruct((3 * panels, rows, LANES), BF16),
        name="pack",
    )(w_gate, w_up, w_down)


def first_product(where, mine, theirs, weights):
    groups, lows, rows, width = mine.shape
    ranks, panels, depth, _ = weights.shape
    used = panels // 3 * 2
    wide = 2 * LANES
    span = width // depth

    def body(where_ref, mine_ref, theirs_ref, w_ref, sent_ref, own_ref):
        acc = jnp.zeros((groups * rows, wide), F32)
        for low in range(lows):
            for flip, ref in enumerate((mine_ref, theirs_ref)):
                core = where_ref[1] if flip == 0 else 1 - where_ref[1]
                at = pl.ds((low * 2 + core) * span, span)
                rhs = jnp.concatenate([w_ref[at, i].reshape(width, LANES) for i in range(2)], 1)
                part = ref[:, low].reshape(groups * rows, width)
                acc = acc + jnp.dot(part, rhs, preferred_element_type=F32)
        sent_ref[...] = acc.astype(BF16).reshape(groups, rows, wide)
        for z in range(groups):

            @pl.when(where_ref[0] == z)
            def _(z=z):
                own_ref[...] = acc[z * rows : (z + 1) * rows]

    return pl.pallas_call(
        body,
        grid_spec=pltpu.PrefetchScalarGridSpec(
            num_scalar_prefetch=1,
            grid=(used // 2,),
            in_specs=[
                pl.BlockSpec(mine.shape, lambda j, s: (0, 0, 0, 0)),
                pl.BlockSpec(theirs.shape, lambda j, s: (0, 0, 0, 0)),
                pl.BlockSpec((ranks, 2, depth, LANES), lambda j, s: (0, j, 0, 0)),
            ],
            out_specs=[
                pl.BlockSpec((groups, rows, wide), lambda j, s: (0, 0, j)),
                pl.BlockSpec((rows, wide), lambda j, s: (0, j)),
            ],
        ),
        out_shape=[
            jax.ShapeDtypeStruct((groups, rows, used * LANES), BF16),
            jax.ShapeDtypeStruct((rows, used * LANES), F32),
        ],
        cost_estimate=pl.CostEstimate(
            flops=2 * groups * rows * ranks * depth * used * LANES, bytes_accessed=5 << 20, transcendentals=0
        ),
        name="first_product",
    )(where, mine, theirs, weights)


def second_product(where, mine, theirs, near, passed, far):
    rows, depth = mine.shape
    ranks, others = far.shape[:2]
    groups = others + 1
    panels = depth // LANES
    quads = ranks // 2

    def body(where_ref, mine_ref, theirs_ref, near_ref, passed_ref, far_ref, out_ref):
        core = where_ref[1]
        left, right = mine_ref[...], theirs_ref[...]
        for s in range(groups):
            own, other = [], []
            for low in range(2):
                if s == 0:
                    own.append(near_ref[core * 2 + low].reshape(depth, LANES))
                    other.append(passed_ref[0, low].reshape(depth, LANES))
                else:
                    own.append(far_ref[core * 2 + low, s - 1])
                    other.append(far_ref[(1 - core) * 2 + low, s - 1])
            part = jnp.dot(left, jnp.concatenate(own, 1), preferred_element_type=F32)
            part = part + jnp.dot(right, jnp.concatenate(other, 1), preferred_element_type=F32)
            out_ref[lax.rem(where_ref[0] + s, groups), 0] = part.astype(BF16)

    return pl.pallas_call(
        body,
        grid_spec=pltpu.PrefetchScalarGridSpec(
            num_scalar_prefetch=1,
            grid=(2,),
            in_specs=[
                pl.BlockSpec(mine.shape, lambda j, s: (0, 0)),
                pl.BlockSpec(mine.shape, lambda j, s: (0, 0)),
                pl.BlockSpec((quads, panels) + near.shape[2:], lambda j, s: (j, 2, 0, 0)),
                pl.BlockSpec((1,) + passed.shape[1:], lambda j, s: (j, 0, 0, 0, 0)),
                pl.BlockSpec((quads,) + far.shape[1:], lambda j, s: (j, 0, 0, 0)),
            ],
            out_specs=pl.BlockSpec((groups, 1, rows, 2 * LANES), lambda j, s: (0, j, 0, 0)),
        ),
        out_shape=jax.ShapeDtypeStruct((groups, 2, rows, 2 * LANES), BF16),
        cost_estimate=pl.CostEstimate(
            flops=2 * rows * 2 * depth * groups * 4 * LANES, bytes_accessed=5 << 20, transcendentals=0
        ),
        name="second_product",
    )(where, mine, theirs, near, passed, far)


def per_device(tokens, w_gate, w_up, w_down, pattern, gate_code):
    zh = lax.axis_index("zh")
    row_count, width = tokens.shape
    block_count = pattern.shape[0]
    block_rows = row_count // block_count
    groups, ranks, size = lax.axis_size("zh"), lax.axis_size("y"), lax.axis_size(EXP)
    quarter = size // groups
    where = jnp.stack([zh, lax.axis_index("c")]).astype(jnp.int32)

    near = lax.all_gather(pack(w_gate, w_up, w_down), "y", axis=0, tiled=False)
    core = lax.axis_index("c")
    blocks = []
    for shift in range(1, groups):
        moves = []
        for z in range(groups):
            for y in range(ranks):
                for c in range(2):
                    bit = y // 2 % 2
                    target = ((z - shift) % groups * ranks + y + 2 * (c - bit)) * 2 + bit
                    moves.append(((z * ranks + y) * 2 + c, target))
        blocks.append(lax.ppermute(w_down, ("zh", "y", "c"), moves))
    far = lax.all_gather(jnp.stack(blocks), "y", axis=0, tiled=False)

    chosen = jnp.where(pattern[0] > 0, 0, 1)
    rows = lax.dynamic_slice_in_dim(tokens, chosen * block_rows, block_rows, 0)
    flags = jnp.repeat(pattern, block_rows).astype(F32)
    row_scale = (gate_code.astype(F32) / 256.0 * flags).astype(BF16).astype(F32)

    swap = []
    for z in range(groups):
        for a in range(groups):
            for b in range(quarter):
                swap.append((z * size + a * quarter + b, a * size + z * quarter + b))
    rows = lax.ppermute(rows, ("zh",) + EXP, swap)
    chips = size // 2
    copies = jnp.broadcast_to(rows[None], (chips,) + rows.shape)
    mine = lax.all_to_all(copies, ("zl", "x"), split_axis=0, concat_axis=0, tiled=True)
    mine = mine.reshape(groups, chips // groups, block_rows, width)
    theirs = lax.ppermute(mine, "c", [(0, 1), (1, 0)])

    sent, own = first_product(where, mine, theirs, near)
    cores = [(0, 1), (1, 0)]
    later, sent = lax.optimization_barrier((near, sent))
    later = later.reshape((2, 2, 2) + near.shape[1:])
    later = lax.dynamic_index_in_dim(later, 1 - core, 1, keepdims=False)[:, :, -(near.shape[1] // 3) :]
    passed = lax.ppermute(later, "c", cores)
    got = lax.all_to_all(sent, "zh", split_axis=0, concat_axis=0, tiled=True)
    total = own
    for k in range(groups):
        total = total + jnp.where(k == zh, 0.0, got[k].astype(F32))
    gate, up = jnp.split(total, 2, 1)
    hidden = (jax.nn.silu(gate) * up).astype(BF16)

    hidden, passed = lax.optimization_barrier((hidden, passed))
    part = second_product(where, hidden, lax.ppermute(hidden, "c", cores), near, passed, far)
    parts = lax.all_to_all(part.reshape(chips, block_rows, width), ("zl", "x"), split_axis=0, concat_axis=0, tiled=True)
    summed = jnp.sum(parts.astype(F32), 0)
    result = row_scale.reshape(block_count, block_rows, 1) * summed[None]
    return result.astype(BF16).reshape(row_count, width)


def solution(mesh):
    wide = Mesh(mesh.devices.reshape(4, 8, 2, 4, 2), ("zh", "y", "zl", "x", "c"))
    in_specs = (
        P(TOK, EXP),
        P(TOK, EXP),
        P(TOK, EXP),
        P(EXP, TOK),
        P(TOK),
        P(TOK),
    )
    return jax.shard_map(
        per_device, mesh=wide, in_specs=in_specs, out_specs=P(TOK, EXP), check_vma=False
    )
```

```python
import jax
import jax.numpy as jnp
from jax import lax
from jax.experimental import pallas as pl
from jax.experimental.pallas import tpu as pltpu
from jax.sharding import Mesh
from jax.sharding import PartitionSpec as P

TOK = ("zh", "y")
EXP = ("zl", "x", "c")
F32, BF16 = jnp.float32, jnp.bfloat16
LANES = 128


def in_vmem(array):
    return pltpu.with_memory_space_constraint(array, pltpu.VMEM)


def pack(w_gate, w_up, w_down):
    rows, cols = w_gate.shape
    panels = cols // LANES

    def body(gate_ref, up_ref, down_ref, out_ref):
        for j in range(panels):
            out_ref[j] = gate_ref[:, j * LANES : (j + 1) * LANES]
            out_ref[panels + j] = up_ref[:, j * LANES : (j + 1) * LANES]
            out_ref[2 * panels + j] = down_ref[j * rows : (j + 1) * rows]

    return pl.pallas_call(
        body,
        out_shape=jax.ShapeDtypeStruct((3 * panels, rows, LANES), BF16),
        name="pack",
    )(w_gate, w_up, w_down)


def first_product(where, mine, theirs, weights):
    groups, lows, rows, width = mine.shape
    ranks, panels, depth, _ = weights.shape
    used = panels // 3 * 2
    wide = 2 * LANES
    span = width // depth

    def body(where_ref, mine_ref, theirs_ref, w_ref, sent_ref, own_ref):
        acc = jnp.zeros((groups * rows, wide), F32)
        for low in range(lows):
            for flip, ref in enumerate((mine_ref, theirs_ref)):
                core = where_ref[1] if flip == 0 else 1 - where_ref[1]
                at = pl.ds((low * 2 + core) * span, span)
                rhs = jnp.concatenate([w_ref[at, i].reshape(width, LANES) for i in range(2)], 1)
                part = ref[:, low].reshape(groups * rows, width)
                acc = acc + jnp.dot(part, rhs, preferred_element_type=F32)
        sent_ref[...] = acc.astype(BF16).reshape(groups, rows, wide)
        for z in range(groups):

            @pl.when(where_ref[0] == z)
            def _(z=z):
                own_ref[...] = acc[z * rows : (z + 1) * rows]

    return pl.pallas_call(
        body,
        grid_spec=pltpu.PrefetchScalarGridSpec(
            num_scalar_prefetch=1,
            grid=(used // 2,),
            in_specs=[
                pl.BlockSpec(memory_space=pltpu.VMEM),
                pl.BlockSpec(memory_space=pltpu.VMEM),
                pl.BlockSpec((ranks, 2, depth, LANES), lambda j, s: (0, j, 0, 0)),
            ],
            out_specs=[
                pl.BlockSpec((groups, rows, wide), lambda j, s: (0, 0, j)),
                pl.BlockSpec((rows, wide), lambda j, s: (0, j)),
            ],
        ),
        out_shape=[
            jax.ShapeDtypeStruct((groups, rows, used * LANES), BF16),
            jax.ShapeDtypeStruct((rows, used * LANES), F32),
        ],
        cost_estimate=pl.CostEstimate(
            flops=2 * groups * rows * ranks * depth * used * LANES, bytes_accessed=5 << 20, transcendentals=0
        ),
        name="first_product",
    )(where, mine, theirs, weights)


def second_product(where, mine, theirs, near, passed, far):
    rows, depth = mine.shape
    ranks, others = far.shape[:2]
    groups = others + 1
    quads = ranks // 2

    def body(where_ref, mine_ref, theirs_ref, near_ref, passed_ref, far_ref, out_ref):
        core = where_ref[1]
        left, right = mine_ref[...], theirs_ref[...]
        for s in range(groups):
            own, other = [], []
            for low in range(2):
                if s == 0:
                    own.append(near_ref[pl.program_id(0) * quads + core * 2 + low].reshape(depth, LANES))
                    other.append(passed_ref[pl.program_id(0), low].reshape(depth, LANES))
                else:
                    own.append(far_ref[core * 2 + low, s - 1])
                    other.append(far_ref[(1 - core) * 2 + low, s - 1])
            part = jnp.dot(left, jnp.concatenate(own, 1), preferred_element_type=F32)
            part = part + jnp.dot(right, jnp.concatenate(other, 1), preferred_element_type=F32)
            out_ref[lax.rem(where_ref[0] + s, groups), 0] = part.astype(BF16)

    return pl.pallas_call(
        body,
        grid_spec=pltpu.PrefetchScalarGridSpec(
            num_scalar_prefetch=1,
            grid=(2,),
            in_specs=[
                pl.BlockSpec(memory_space=pltpu.VMEM),
                pl.BlockSpec(memory_space=pltpu.VMEM),
                pl.BlockSpec(memory_space=pltpu.VMEM),
                pl.BlockSpec(memory_space=pltpu.VMEM),
                pl.BlockSpec((quads,) + far.shape[1:], lambda j, s: (j, 0, 0, 0)),
            ],
            out_specs=pl.BlockSpec((groups, 1, rows, 2 * LANES), lambda j, s: (0, j, 0, 0)),
        ),
        out_shape=jax.ShapeDtypeStruct((groups, 2, rows, 2 * LANES), BF16),
        cost_estimate=pl.CostEstimate(
            flops=2 * rows * 2 * depth * groups * 4 * LANES, bytes_accessed=5 << 20, transcendentals=0
        ),
        name="second_product",
    )(where, mine, theirs, near, passed, far)


def per_device(tokens, w_gate, w_up, w_down, pattern, gate_code):
    zh = lax.axis_index("zh")
    row_count, width = tokens.shape
    block_count = pattern.shape[0]
    block_rows = row_count // block_count
    groups, ranks, size = lax.axis_size("zh"), lax.axis_size("y"), lax.axis_size(EXP)
    quarter = size // groups
    where = jnp.stack([zh, lax.axis_index("c")]).astype(jnp.int32)

    near = lax.all_gather(pack(w_gate, w_up, w_down), "y", axis=0, tiled=False)
    core = lax.axis_index("c")
    blocks = []
    for shift in range(1, groups):
        moves = []
        for z in range(groups):
            for y in range(ranks):
                for c in range(2):
                    bit = y // 2 % 2
                    target = ((z - shift) % groups * ranks + y + 2 * (c - bit)) * 2 + bit
                    moves.append(((z * ranks + y) * 2 + c, target))
        blocks.append(lax.ppermute(w_down, ("zh", "y", "c"), moves))
    far = lax.all_gather(jnp.stack(blocks), "y", axis=0, tiled=False)

    chosen = jnp.where(pattern[0] > 0, 0, 1)
    rows = lax.dynamic_slice_in_dim(tokens, chosen * block_rows, block_rows, 0)
    flags = jnp.repeat(pattern, block_rows).astype(F32)
    row_scale = (gate_code.astype(F32) / 256.0 * flags).astype(BF16).astype(F32)

    swap = []
    for z in range(groups):
        for a in range(groups):
            for b in range(quarter):
                swap.append((z * size + a * quarter + b, a * size + z * quarter + b))
    rows = lax.ppermute(rows, ("zh",) + EXP, swap)
    chips = size // 2
    copies = jnp.broadcast_to(rows[None], (chips,) + rows.shape)
    mine = lax.all_to_all(copies, ("zl", "x"), split_axis=0, concat_axis=0, tiled=True)
    mine = mine.reshape(groups, chips // groups, block_rows, width)
    theirs = lax.ppermute(mine, "c", [(0, 1), (1, 0)])

    sent, own = first_product(where, in_vmem(mine), in_vmem(theirs), near)
    cores = [(0, 1), (1, 0)]
    later, sent = lax.optimization_barrier((near, sent))
    later = later[:, -(near.shape[1] // 3) :]
    other_half = lax.dynamic_index_in_dim(later.reshape((2, 2, 2) + later.shape[1:]), 1 - core, 1, keepdims=False)
    passed = lax.ppermute(other_half, "c", cores)
    got = lax.all_to_all(sent, "zh", split_axis=0, concat_axis=0, tiled=True)
    total = own
    for k in range(groups):
        total = total + jnp.where(k == zh, 0.0, got[k].astype(F32))
    gate, up = jnp.split(total, 2, 1)
    hidden = (jax.nn.silu(gate) * up).astype(BF16)

    hidden, passed = lax.optimization_barrier((hidden, passed))
    theirs = lax.ppermute(hidden, "c", cores)
    part = second_product(where, *map(in_vmem, (hidden, theirs, later, passed)), far)
    parts = lax.all_to_all(part.reshape(chips, block_rows, width), ("zl", "x"), split_axis=0, concat_axis=0, tiled=True)
    summed = jnp.sum(parts.astype(F32), 0)
    result = row_scale.reshape(block_count, block_rows, 1) * summed[None]
    return result.astype(BF16).reshape(row_count, width)


def solution(mesh):
    wide = Mesh(mesh.devices.reshape(4, 8, 2, 4, 2), ("zh", "y", "zl", "x", "c"))
    in_specs = (
        P(TOK, EXP),
        P(TOK, EXP),
        P(TOK, EXP),
        P(EXP, TOK),
        P(TOK),
        P(TOK),
    )
    return jax.shard_map(
        per_device, mesh=wide, in_specs=in_specs, out_specs=P(TOK, EXP), check_vma=False
    )
```

```python
import jax
import jax.numpy as jnp
from jax import lax
from jax.experimental import pallas as pl
from jax.experimental.pallas import tpu as pltpu
from jax.sharding import Mesh
from jax.sharding import PartitionSpec as P

TOK = ("zh", "y")
EXP = ("zl", "x", "c")
F32, BF16 = jnp.float32, jnp.bfloat16
LANES = 128


def in_vmem(array):
    return pltpu.with_memory_space_constraint(array, pltpu.VMEM)


def pack(w_gate, w_up, w_down):
    rows, cols = w_gate.shape
    panels = cols // LANES

    def body(gate_ref, up_ref, down_ref, out_ref):
        for j in range(panels):
            out_ref[j] = gate_ref[:, j * LANES : (j + 1) * LANES]
            out_ref[panels + j] = up_ref[:, j * LANES : (j + 1) * LANES]
            out_ref[2 * panels + j] = down_ref[j * rows : (j + 1) * rows]

    return pl.pallas_call(
        body,
        out_shape=jax.ShapeDtypeStruct((3 * panels, rows, LANES), BF16),
        name="pack",
    )(w_gate, w_up, w_down)


def first_product(where, mine, theirs, weights):
    groups, lows, rows, width = mine.shape
    ranks, panels, depth, _ = weights.shape
    used = panels // 3 * 2
    wide = 2 * LANES
    span = width // depth

    def body(where_ref, mine_ref, theirs_ref, w_ref, sent_ref, own_ref):
        acc = jnp.zeros((groups * rows, wide), F32)
        for low in range(lows):
            for flip, ref in enumerate((mine_ref, theirs_ref)):
                core = where_ref[1] if flip == 0 else 1 - where_ref[1]
                at = pl.ds((low * 2 + core) * span, span)
                rhs = jnp.concatenate([w_ref[at, i].reshape(width, LANES) for i in range(2)], 1)
                part = ref[:, low].reshape(groups * rows, width)
                acc = acc + jnp.dot(part, rhs, preferred_element_type=F32)
        sent_ref[...] = acc.astype(BF16).reshape(groups, rows, wide)
        for z in range(groups):

            @pl.when(where_ref[0] == z)
            def _(z=z):
                own_ref[...] = acc[z * rows : (z + 1) * rows]

    return pl.pallas_call(
        body,
        grid_spec=pltpu.PrefetchScalarGridSpec(
            num_scalar_prefetch=1,
            grid=(used // 2,),
            in_specs=[
                pl.BlockSpec(memory_space=pltpu.VMEM),
                pl.BlockSpec(memory_space=pltpu.VMEM),
                pl.BlockSpec((ranks, 2, depth, LANES), lambda j, s: (0, j, 0, 0)),
            ],
            out_specs=[
                pl.BlockSpec((groups, rows, wide), lambda j, s: (0, 0, j)),
                pl.BlockSpec((rows, wide), lambda j, s: (0, j)),
            ],
        ),
        out_shape=[
            jax.ShapeDtypeStruct((groups, rows, used * LANES), BF16),
            jax.ShapeDtypeStruct((rows, used * LANES), F32),
        ],
        cost_estimate=pl.CostEstimate(
            flops=2 * groups * rows * ranks * depth * used * LANES, bytes_accessed=5 << 20, transcendentals=0
        ),
        name="first_product",
    )(where, mine, theirs, weights)


def second_product(where, mine, theirs, near, passed, far):
    rows, depth = mine.shape
    ranks, others = far.shape[:2]
    groups = others + 1
    quads = ranks // 2

    def body(where_ref, mine_ref, theirs_ref, near_ref, passed_ref, far_ref, out_ref):
        core = where_ref[1]
        both = jnp.concatenate([mine_ref[...], theirs_ref[...]], 1)
        for s in range(groups):
            own, other = [], []
            for low in range(2):
                if s == 0:
                    own.append(near_ref[pl.program_id(0) * quads + core * 2 + low].reshape(depth, LANES))
                    other.append(passed_ref[pl.program_id(0), low].reshape(depth, LANES))
                else:
                    own.append(far_ref[core * 2 + low, s - 1])
                    other.append(far_ref[(1 - core) * 2 + low, s - 1])
            rhs = jnp.concatenate([jnp.concatenate(own, 1), jnp.concatenate(other, 1)], 0)
            part = jnp.dot(both, rhs, preferred_element_type=F32)
            out_ref[lax.rem(where_ref[0] + s, groups), pl.program_id(0)] = part.astype(BF16)

    return pl.pallas_call(
        body,
        grid_spec=pltpu.PrefetchScalarGridSpec(
            num_scalar_prefetch=1,
            grid=(2,),
            in_specs=[
                pl.BlockSpec(memory_space=pltpu.VMEM),
                pl.BlockSpec(memory_space=pltpu.VMEM),
                pl.BlockSpec(memory_space=pltpu.VMEM),
                pl.BlockSpec(memory_space=pltpu.VMEM),
                pl.BlockSpec((quads,) + far.shape[1:], lambda j, s: (j, 0, 0, 0)),
            ],
            out_specs=pl.BlockSpec(memory_space=pltpu.VMEM),
        ),
        out_shape=pltpu.VMEM((groups, 2, rows, 2 * LANES), BF16),
        cost_estimate=pl.CostEstimate(
            flops=2 * rows * 2 * depth * groups * 4 * LANES, bytes_accessed=5 << 20, transcendentals=0
        ),
        name="second_product",
    )(where, mine, theirs, near, passed, far)


def per_device(tokens, w_gate, w_up, w_down, pattern, gate_code):
    zh = lax.axis_index("zh")
    row_count, width = tokens.shape
    block_count = pattern.shape[0]
    block_rows = row_count // block_count
    groups, ranks, size = lax.axis_size("zh"), lax.axis_size("y"), lax.axis_size(EXP)
    quarter = size // groups
    where = jnp.stack([zh, lax.axis_index("c")]).astype(jnp.int32)

    near = lax.all_gather(pack(w_gate, w_up, w_down), "y", axis=0, tiled=False)
    core = lax.axis_index("c")
    blocks = []
    for shift in range(1, groups):
        moves = []
        for z in range(groups):
            for y in range(ranks):
                for c in range(2):
                    bit = y // 2 % 2
                    target = ((z - shift) % groups * ranks + y + 2 * (c - bit)) * 2 + bit
                    moves.append(((z * ranks + y) * 2 + c, target))
        blocks.append(lax.ppermute(w_down, ("zh", "y", "c"), moves))
    far = lax.all_gather(jnp.stack(blocks), "y", axis=0, tiled=False)

    chosen = jnp.where(pattern[0] > 0, 0, 1)
    rows = lax.dynamic_slice_in_dim(tokens, chosen * block_rows, block_rows, 0)
    flags = jnp.repeat(pattern, block_rows).astype(F32)
    row_scale = (gate_code.astype(F32) / 256.0 * flags).astype(BF16).astype(F32)

    swap = []
    for z in range(groups):
        for a in range(groups):
            for b in range(quarter):
                swap.append((z * size + a * quarter + b, a * size + z * quarter + b))
    rows = lax.ppermute(rows, ("zh",) + EXP, swap)
    chips = size // 2
    copies = jnp.broadcast_to(rows[None], (chips,) + rows.shape)
    mine = lax.all_to_all(copies, ("zl", "x"), split_axis=0, concat_axis=0, tiled=True)
    mine = mine.reshape(groups, chips // groups, block_rows, width)
    theirs = lax.ppermute(mine, "c", [(0, 1), (1, 0)])

    sent, own = first_product(where, in_vmem(mine), in_vmem(theirs), near)
    cores = [(0, 1), (1, 0)]
    later, sent = lax.optimization_barrier((near, sent))
    later = later[:, -(near.shape[1] // 3) :]
    other_half = lax.dynamic_index_in_dim(later.reshape((2, 2, 2) + later.shape[1:]), 1 - core, 1, keepdims=False)
    passed = lax.ppermute(other_half, "c", cores)
    got = lax.all_to_all(sent, "zh", split_axis=0, concat_axis=0, tiled=True)
    total = own
    for k in range(groups):
        total = total + jnp.where(k == zh, 0.0, got[k].astype(F32))
    gate, up = jnp.split(total, 2, 1)
    hidden = (jax.nn.silu(gate) * up).astype(BF16)

    hidden, passed = lax.optimization_barrier((hidden, passed))
    theirs = lax.ppermute(hidden, "c", cores)
    part = second_product(where, *map(in_vmem, (hidden, theirs, later, passed)), far)
    parts = lax.all_to_all(part.reshape(chips, block_rows, width), ("zl", "x"), split_axis=0, concat_axis=0, tiled=True)
    summed = jnp.sum(parts.astype(F32), 0)
    result = row_scale.reshape(block_count, block_rows, 1) * summed[None]
    return result.astype(BF16).reshape(row_count, width)


def solution(mesh):
    wide = Mesh(mesh.devices.reshape(4, 8, 2, 4, 2), ("zh", "y", "zl", "x", "c"))
    in_specs = (
        P(TOK, EXP),
        P(TOK, EXP),
        P(TOK, EXP),
        P(EXP, TOK),
        P(TOK),
        P(TOK),
    )
    return jax.shard_map(
        per_device, mesh=wide, in_specs=in_specs, out_specs=P(TOK, EXP), check_vma=False
    )
```

```python
import jax
import jax.numpy as jnp
from jax import lax
from jax.experimental import pallas as pl
from jax.experimental.pallas import tpu as pltpu
from jax.sharding import Mesh
from jax.sharding import PartitionSpec as P

TOK = ("zh", "y")
EXP = ("zl", "x", "c")
F32, BF16 = jnp.float32, jnp.bfloat16
LANES = 128


def in_vmem(array):
    return pltpu.with_memory_space_constraint(array, pltpu.VMEM)


def pack(w_gate, w_up, w_down):
    rows, cols = w_gate.shape
    panels = cols // LANES

    def body(gate_ref, up_ref, down_ref, out_ref, held_ref, in_sems, out_sems):
        loads = []
        for j in range(panels):
            at = pl.ds(j * LANES, LANES)
            for part, source in enumerate((gate_ref.at[:, at], up_ref.at[:, at], down_ref.at[pl.ds(j * rows, rows)])):
                k = part * panels + j
                loads.append((k, pltpu.make_async_copy(source, held_ref.at[k], in_sems.at[k])))
        for _, load in loads:
            load.start()
        stores = []
        for k, load in loads:
            load.wait()
            store = pltpu.make_async_copy(held_ref.at[k], out_ref.at[k], out_sems.at[k])
            store.start()
            stores.append(store)
        for store in stores:
            store.wait()

    return pl.pallas_call(
        body,
        in_specs=[pl.BlockSpec(memory_space=pl.ANY)] * 3,
        out_specs=pl.BlockSpec(memory_space=pl.ANY),
        out_shape=jax.ShapeDtypeStruct((3 * panels, rows, LANES), BF16),
        scratch_shapes=[
            pltpu.VMEM((3 * panels, rows, LANES), BF16),
            pltpu.SemaphoreType.DMA((3 * panels,)),
            pltpu.SemaphoreType.DMA((3 * panels,)),
        ],
        name="pack",
    )(w_gate, w_up, w_down)


def first_product(where, mine, theirs, weights):
    groups, lows, rows, width = mine.shape
    ranks, panels, depth, _ = weights.shape
    used = panels // 3 * 2
    wide = 2 * LANES
    span = width // depth

    def body(where_ref, mine_ref, theirs_ref, w_ref, sent_ref, own_ref):
        acc = jnp.zeros((groups * rows, wide), F32)
        for low in range(lows):
            for flip, ref in enumerate((mine_ref, theirs_ref)):
                core = where_ref[1] if flip == 0 else 1 - where_ref[1]
                at = pl.ds((low * 2 + core) * span, span)
                rhs = jnp.concatenate([w_ref[at, i].reshape(width, LANES) for i in range(2)], 1)
                part = ref[:, low].reshape(groups * rows, width)
                acc = acc + jnp.dot(part, rhs, preferred_element_type=F32)
        sent_ref[...] = acc.astype(BF16).reshape(groups, rows, wide)
        for z in range(groups):

            @pl.when(where_ref[0] == z)
            def _(z=z):
                own_ref[...] = acc[z * rows : (z + 1) * rows]

    return pl.pallas_call(
        body,
        grid_spec=pltpu.PrefetchScalarGridSpec(
            num_scalar_prefetch=1,
            grid=(used // 2,),
            in_specs=[
                pl.BlockSpec(memory_space=pltpu.VMEM),
                pl.BlockSpec(memory_space=pltpu.VMEM),
                pl.BlockSpec((ranks, 2, depth, LANES), lambda j, s: (0, j, 0, 0)),
            ],
            out_specs=[
                pl.BlockSpec((groups, rows, wide), lambda j, s: (0, 0, j)),
                pl.BlockSpec((rows, wide), lambda j, s: (0, j)),
            ],
        ),
        out_shape=[
            jax.ShapeDtypeStruct((groups, rows, used * LANES), BF16),
            jax.ShapeDtypeStruct((rows, used * LANES), F32),
        ],
        cost_estimate=pl.CostEstimate(
            flops=2 * groups * rows * ranks * depth * used * LANES, bytes_accessed=5 << 20, transcendentals=0
        ),
        name="first_product",
    )(where, mine, theirs, weights)


def second_product(where, mine, theirs, near, passed, far):
    rows, depth = mine.shape
    ranks, others = far.shape[:2]
    groups = others + 1
    quads = ranks // 2

    def body(where_ref, mine_ref, theirs_ref, near_ref, passed_ref, far_ref, out_ref):
        core = where_ref[1]
        both = jnp.concatenate([mine_ref[...], theirs_ref[...]], 1)
        for s in range(groups):
            own, other = [], []
            for low in range(2):
                if s == 0:
                    own.append(near_ref[pl.program_id(0) * quads + core * 2 + low].reshape(depth, LANES))
                    other.append(passed_ref[pl.program_id(0), low].reshape(depth, LANES))
                else:
                    own.append(far_ref[core * 2 + low, s - 1])
                    other.append(far_ref[(1 - core) * 2 + low, s - 1])
            rhs = jnp.concatenate([jnp.concatenate(own, 1), jnp.concatenate(other, 1)], 0)
            part = jnp.dot(both, rhs, preferred_element_type=F32)
            out_ref[lax.rem(where_ref[0] + s, groups), pl.program_id(0)] = part.astype(BF16)

    return pl.pallas_call(
        body,
        grid_spec=pltpu.PrefetchScalarGridSpec(
            num_scalar_prefetch=1,
            grid=(2,),
            in_specs=[
                pl.BlockSpec(memory_space=pltpu.VMEM),
                pl.BlockSpec(memory_space=pltpu.VMEM),
                pl.BlockSpec(memory_space=pltpu.VMEM),
                pl.BlockSpec(memory_space=pltpu.VMEM),
                pl.BlockSpec((quads,) + far.shape[1:], lambda j, s: (j, 0, 0, 0)),
            ],
            out_specs=pl.BlockSpec(memory_space=pltpu.VMEM),
        ),
        out_shape=pltpu.VMEM((groups, 2, rows, 2 * LANES), BF16),
        cost_estimate=pl.CostEstimate(
            flops=2 * rows * 2 * depth * groups * 4 * LANES, bytes_accessed=5 << 20, transcendentals=0
        ),
        name="second_product",
    )(where, mine, theirs, near, passed, far)


def per_device(tokens, w_gate, w_up, w_down, pattern, gate_code):
    zh = lax.axis_index("zh")
    row_count, width = tokens.shape
    block_count = pattern.shape[0]
    block_rows = row_count // block_count
    groups, ranks, size = lax.axis_size("zh"), lax.axis_size("y"), lax.axis_size(EXP)
    quarter = size // groups
    where = jnp.stack([zh, lax.axis_index("c")]).astype(jnp.int32)

    near = lax.all_gather(pack(w_gate, w_up, w_down), "y", axis=0, tiled=False)
    core = lax.axis_index("c")
    blocks = []
    for shift in range(1, groups):
        moves = []
        for z in range(groups):
            for y in range(ranks):
                for c in range(2):
                    bit = y // 2 % 2
                    target = ((z - shift) % groups * ranks + y + 2 * (c - bit)) * 2 + bit
                    moves.append(((z * ranks + y) * 2 + c, target))
        blocks.append(lax.ppermute(w_down, ("zh", "y", "c"), moves))
    far = lax.all_gather(jnp.stack(blocks), "y", axis=0, tiled=False)

    chosen = jnp.where(pattern[0] > 0, 0, 1)
    rows = lax.dynamic_slice_in_dim(tokens, chosen * block_rows, block_rows, 0)
    flags = jnp.repeat(pattern, block_rows).astype(F32)
    row_scale = (gate_code.astype(F32) / 256.0 * flags).astype(BF16).astype(F32)

    swap = []
    for z in range(groups):
        for a in range(groups):
            for b in range(quarter):
                swap.append((z * size + a * quarter + b, a * size + z * quarter + b))
    rows = lax.ppermute(rows, ("zh",) + EXP, swap)
    chips = size // 2
    copies = jnp.broadcast_to(rows[None], (chips,) + rows.shape)
    mine = lax.all_to_all(copies, ("zl", "x"), split_axis=0, concat_axis=0, tiled=True)
    mine = mine.reshape(groups, chips // groups, block_rows, width)
    theirs = lax.ppermute(mine, "c", [(0, 1), (1, 0)])

    sent, own = first_product(where, in_vmem(mine), in_vmem(theirs), near)
    cores = [(0, 1), (1, 0)]
    later, sent = lax.optimization_barrier((near, sent))
    later = later[:, -(near.shape[1] // 3) :]
    other_half = lax.dynamic_index_in_dim(later.reshape((2, 2, 2) + later.shape[1:]), 1 - core, 1, keepdims=False)
    passed = lax.ppermute(other_half, "c", cores)
    got = lax.all_to_all(sent, "zh", split_axis=0, concat_axis=0, tiled=True)
    total = own
    for k in range(groups):
        total = total + jnp.where(k == zh, 0.0, got[k].astype(F32))
    gate, up = jnp.split(total, 2, 1)
    hidden = (jax.nn.silu(gate) * up).astype(BF16)

    hidden, passed = lax.optimization_barrier((hidden, passed))
    theirs = lax.ppermute(hidden, "c", cores)
    part = second_product(where, *map(in_vmem, (hidden, theirs, later, passed)), far)
    parts = lax.all_to_all(part.reshape(chips, block_rows, width), ("zl", "x"), split_axis=0, concat_axis=0, tiled=True)
    summed = jnp.sum(parts.astype(F32), 0)
    result = row_scale.reshape(block_count, block_rows, 1) * summed[None]
    return result.astype(BF16).reshape(row_count, width)


def solution(mesh):
    wide = Mesh(mesh.devices.reshape(4, 8, 2, 4, 2), ("zh", "y", "zl", "x", "c"))
    in_specs = (
        P(TOK, EXP),
        P(TOK, EXP),
        P(TOK, EXP),
        P(EXP, TOK),
        P(TOK),
        P(TOK),
    )
    return jax.shard_map(
        per_device, mesh=wide, in_specs=in_specs, out_specs=P(TOK, EXP), check_vma=False
    )
```
